32 devices in a mesh: wide: 8 (over z, y), narrow: 4 (over x, core).
Axes of the slice: x: 2, y: 2, z: 4, core: 2. Of those that a mesh axis runs over, the one named last changes fastest.
Arguments:
- tokens: bfloat16 [32768, 768], P(('wide', 'narrow')), may hold values from -6 to 6
- segment_ids: int32 [32768], P(('wide', 'narrow')), may hold values from 0 to 4, as said below
- cotangent: bfloat16 [32768, 768], P(('wide', 'narrow')), may hold values from -6 to 6
- ln1_gain: bfloat16 [768], P('wide'), may hold values from 0.5 to 1.5
- ln1_bias: bfloat16 [768], P('wide'), may hold values from -1 to 1
- qkv_weight: bfloat16 [768, 2304], P('wide'), may hold values from -0.3125 to 0.3125
- qv_bias: bfloat16 [1536], P('wide'), may hold values from -1 to 1
- out_weight: bfloat16 [768, 768], P('wide'), may hold values from -0.625 to 0.625
- out_bias: bfloat16 [768], P('wide'), may hold values from -1 to 1
- ln2_gain: bfloat16 [768], P('wide'), may hold values from 0.5 to 1.5
- ln2_bias: bfloat16 [768], P('wide'), may hold values from -1 to 1
- up_weight: bfloat16 [768, 3072], P('wide'), may hold values from -0.21875 to 0.21875
- up_bias: bfloat16 [3072], P('wide'), may hold values from -1 to 1
- down_weight: bfloat16 [3072, 768], P('wide'), may hold values from -0.109375 to 0.109375
- down_bias: bfloat16 [768], P('wide'), may hold values from -1 to 1
Outputs:
- output: bfloat16 [32768, 768], P(('wide', 'narrow'))
- tokens_grad: float32 [32768, 768], P(('wide', 'narrow'))
- ln1_gain_grad: float32 [768], P('wide')
- ln1_bias_grad: float32 [768], P('wide')
- qkv_weight_grad: float32 [768, 2304], P('wide')
- qv_bias_grad: float32 [1536], P('wide')
- out_weight_grad: float32 [768, 768], P('wide')
- out_bias_grad: float32 [768], P('wide')
- ln2_gain_grad: float32 [768], P('wide')
- ln2_bias_grad: float32 [768], P('wide')
- up_weight_grad: float32 [768, 3072], P('wide')
- up_bias_grad: float32 [3072], P('wide')
- down_weight_grad: float32 [3072, 768], P('wide')
- down_bias_grad: float32 [768], P('wide')
The draws below stay inside these ranges and needn't reach their ends.
Inputs may be any that keep to these rules, and one draw needn't show every extreme that they name: In each sequence of 1024 rows, segment_ids at position p is (offset + p) // 256 for one offset of 1 to 255 of that sequence.
All inputs are finite; a program needn't handle non-finite values.
Results may differ from the reference program's by a relative error of at most 0.017.
Values may be sent and summed in bfloat16 or wider, within the bound.
No kernel may reach another device: no remote copies, remote signals or barrier semaphores. Data moves between devices by JAX's collectives and lax.ppermute only.
A program may use at most 192 MiB of HBM per device.

```python
import jax
import jax.numpy as jnp
from jax import lax

D = 768
HEADS = 16
HEAD_DIM = 48
FF = 3072
IMAGE = 256
LENGTH = 1024
TOKENS = 32768


def draw_segment_ids(key, part):
    seq_count = TOKENS // LENGTH
    offsets = jax.random.randint(key, (seq_count, 1), 1, IMAGE, dtype=jnp.int32)
    position = jnp.arange(LENGTH, dtype=jnp.int32)[None, :]
    return ((offsets + position) // IMAGE).reshape(TOKENS).astype(jnp.int32)


def raised(values, stream_key, source, target, blocks, factor):
    owner, partner = [(jnp.arange(values.shape[dim]) // (values.shape[dim] // blocks)).reshape([-1 if axis == dim else 1 for axis in range(values.ndim)]) for dim in (source, target)]
    chosen = jax.random.permutation(stream_key, blocks)[partner]
    strong = (owner == chosen) | (owner == (partner + blocks // 2) % blocks)
    return jnp.where(strong, factor * values, values)


def levels(stream_key, shape, shards, least, high):
    def one(dim, blocks):
        heights = jax.random.uniform(jax.random.fold_in(jax.random.fold_in(stream_key, 6), dim), (blocks,), jnp.float32, least / len(shards), high / len(shards))
        return jnp.repeat(jnp.exp(heights), shape[dim] // blocks).reshape((-1,) + (1,) * (len(shape) - dim - 1))

    level = one(*shards[0])
    for cut in shards[1:]:
        level = level * one(*cut)
    return level


def normal_values(own_key, extent, spread, bound, cuts=(), kind=jnp.bfloat16):
    level = levels(own_key, extent, cuts, -0.22, 0.18) if cuts else 1.0
    entries = jax.random.normal(own_key, extent, jnp.float32) * spread * level
    return jnp.minimum(jnp.maximum(entries, -bound), bound).astype(kind)


def heavy_noise(own_key, shape, spread, bound, cuts, heavy, kind=jnp.bfloat16):
    values = spread * jax.random.normal(own_key, shape, jnp.float32)
    if cuts:
        values = values * levels(own_key, shape, cuts, -0.22, 0.18)
    return jnp.clip(raised(values, jax.random.fold_in(own_key, 3), *heavy), -bound, bound).astype(kind)


def setup_inputs(seed: int = 0) -> dict:
    key_list = jax.random.split(jax.random.key(seed), 16)
    return {
        "tokens": normal_values(key_list[0], (TOKENS, D), 1.0, 6.0, ((0, 32),)),
        "segment_ids": draw_segment_ids(jax.random.fold_in(key_list[15], 71), 0),
        "cotangent": heavy_noise(key_list[2], (TOKENS, D), 1.0, 6.0, ((0, 32),), (0, 1, 32, 2.75)),
        "ln1_gain": jnp.clip(1.0 + 0.1 * jax.random.normal(key_list[3], (D,), jnp.float32), 0.5, 1.5).astype(jnp.bfloat16),
        "ln1_bias": normal_values(key_list[4], (D,), 0.2, 1.0, ((0, 8),)),
        "qkv_weight": normal_values(key_list[5], (D, 3 * D), (D // 2) ** -0.5, 0.3125, ((0, 8),)),
        "qv_bias": normal_values(key_list[6], (2 * D,), 0.2, 1.0, ((0, 8),)),
        "out_weight": normal_values(key_list[7], (D, D), (D // 8) ** -0.5, 0.625, ((0, 8),)),
        "out_bias": normal_values(key_list[8], (D,), 0.2, 1.0, ((0, 8),)),
        "ln2_gain": jnp.clip(1.0 + 0.1 * jax.random.normal(key_list[9], (D,), jnp.float32), 0.5, 1.5).astype(jnp.bfloat16),
        "ln2_bias": normal_values(key_list[10], (D,), 0.2, 1.0, ((0, 8),)),
        "up_weight": normal_values(key_list[11], (D, FF), D ** -0.5, 0.21875, ((0, 8),)),
        "up_bias": normal_values(key_list[12], (FF,), 0.2, 1.0, ((0, 8),)),
        "down_weight": normal_values(key_list[13], (FF, D), FF ** -0.5, 0.109375, ((0, 8),)),
        "down_bias": normal_values(key_list[14], (D,), 0.2, 1.0, ((0, 8),)),
    }


@jax.custom_vjp
def low(v):
    return lax.optimization_barrier(v.astype(jnp.bfloat16)).astype(jnp.float32)

@jax.custom_vjp
def low_back(v):
    return v

def low_keep(v):
    return (low(v), None)

def low_pass(kept, grad):
    return (grad,)

def back_keep(v):
    return (v, None)

def back_low(kept, grad):
    return (low(grad),)
low.defvjp(low_keep, low_pass)
low_back.defvjp(back_keep, back_low)
EPSILON = 1e-06
NEGATIVE = -1e+30

def matmul(left, right):
    return jnp.dot(left, right, precision=lax.Precision.HIGHEST, preferred_element_type=jnp.float32)

def normalized_rows(value, gain, shift):
    centred = value - lax.optimization_barrier(jnp.mean(value, axis=-1, keepdims=True))
    inverse = lax.rsqrt(lax.optimization_barrier(jnp.mean(centred * centred, axis=-1, keepdims=True)) + EPSILON)
    return centred * inverse * gain + shift

def sequence_layer(inputs, segments, params):
    gain_one, shift_one, mix_weight, mix_bias, proj_weight, proj_bias, gain_two, shift_two, up_weight, up_bias, down_weight, down_bias = params
    length = inputs.shape[0]
    first_normalized = low(normalized_rows(inputs, gain_one, shift_one))
    blanks = jnp.zeros((D,), jnp.float32)
    bias_all = jnp.concatenate([mix_bias[:D], blanks, mix_bias[D:]])
    qkv = low(low_back(matmul(first_normalized, mix_weight) + bias_all))
    split = jnp.transpose(qkv.reshape(length, 3, HEADS, HEAD_DIM), (1, 2, 0, 3))
    queries, keys, values = (split[0], split[1], split[2])
    scores = jnp.einsum('hqd,hkd->hqk', queries, keys, precision=lax.Precision.HIGHEST) * HEAD_DIM ** (-0.5)
    scores = low_back(scores)
    same = segments[:, None] == segments[None, :]
    scores = jnp.where(same[None], scores, NEGATIVE)
    highest = lax.optimization_barrier(jnp.max(scores, axis=-1, keepdims=True))
    expo = jnp.exp(scores - highest)
    probs = low(expo / lax.optimization_barrier(jnp.sum(expo, axis=-1, keepdims=True)))
    attended = jnp.einsum('hqk,hkd->hqd', probs, values, precision=lax.Precision.HIGHEST)
    attended = low(low_back(jnp.transpose(attended, (1, 0, 2)).reshape(length, D)))
    after = inputs + low_back(matmul(attended, proj_weight) + proj_bias)
    second_normalized = low(normalized_rows(after, gain_two, shift_two))
    pre = low_back(matmul(second_normalized, up_weight) + up_bias)
    hidden = low(jax.nn.gelu(pre, approximate=False))
    return after + low_back(matmul(hidden, down_weight) + down_bias)

def reference(tokens, segment_ids, cotangent, ln1_gain, ln1_bias, qkv_weight, qv_bias, out_weight, out_bias, ln2_gain, ln2_bias, up_weight, up_bias, down_weight, down_bias):
    params = tuple((p.astype(jnp.float32) for p in (ln1_gain, ln1_bias, qkv_weight, qv_bias, out_weight, out_bias, ln2_gain, ln2_bias, up_weight, up_bias, down_weight, down_bias)))
    seq_count = tokens.shape[0] // LENGTH
    inputs = tokens.astype(jnp.float32).reshape(seq_count, LENGTH, D)
    segments = segment_ids.astype(jnp.int32).reshape(seq_count, LENGTH)
    upstream = cotangent.astype(jnp.float32).reshape(seq_count, LENGTH, D)

    def one_sequence(totals, item):
        seq_input, seq_segments, seq_upstream = item

        def layer_of(values, weights):
            return sequence_layer(values, seq_segments, weights)
        result, puller = jax.vjp(layer_of, seq_input, params)
        input_grad, param_grads = puller(seq_upstream)
        totals = jax.tree.map(lambda first, second: first + second, totals, param_grads)
        return (totals, (result.astype(jnp.bfloat16), input_grad))
    start = tuple((jnp.zeros_like(p) for p in params))
    totals, (results, input_grads) = lax.scan(one_sequence, start, (inputs, segments, upstream))
    return (results.reshape(tokens.shape), input_grads.reshape(tokens.shape), totals[0], totals[1], totals[2], totals[3], totals[4], totals[5], totals[6], totals[7], totals[8], totals[9], totals[10], totals[11])
```

```python
import functools
import jax
import jax.numpy as jnp
from jax import lax
from jax.experimental import pallas as pl
from jax.experimental.pallas import tpu as pltpu
from jax.sharding import PartitionSpec as P

D = 768
HEADS = 16
HEAD_DIM = 48
LENGTH = 1024
IMAGE = 256
TILES = LENGTH // IMAGE
EPSILON = 1e-06
LOG2E = 1.4426950408889634
SCALE2 = HEAD_DIM ** (-0.5) * LOG2E
f32 = jnp.float32
bf16 = jnp.bfloat16
FULL = pl.Buffered(1)
FF = 4 * D
SIZES = (("g1", D), ("b1", D), ("bq", 3 * D), ("bo", D), ("g2", D), ("b2", D), ("bu", FF), ("bd", D))
SPOTS = {}
TOTAL = 0
for NAME, SIZE in SIZES:
    SPOTS[NAME] = (TOTAL, SIZE)
    TOTAL += SIZE


def vec(ref, name, begin=0, size=None):
    at, full = SPOTS[name]
    return ref[:, at + begin:at + begin + (full if size is None else size)]


def whole(shape):
    return pl.BlockSpec(shape, lambda *_: (0,) * len(shape), pipeline_mode=FULL)


def rows(width):
    return pl.BlockSpec((IMAGE, width), lambda b, *_: (b, 0))


def kept(shape):
    return pl.BlockSpec(shape, lambda *_: (0,) * len(shape))


def dot(left, right, over):
    return lax.dot_general(left, right, ((over[0], over[1]), ((), ())), preferred_element_type=f32)


NN = ((1,), (0,))
NT = ((1,), (1,))
TN = ((0,), (0,))


def window(head):
    first = head * HEAD_DIM
    start = first // 128 * 128
    width = 128 if first + HEAD_DIM <= start + 128 else 256
    return first, start, width


def lane_mask(first, start, width):
    lane = lax.broadcasted_iota(jnp.int32, (1, width), 1) + start
    return (lane >= first) & (lane < first + HEAD_DIM)


def same_image(block, shift):
    size = IMAGE - shift
    row = lax.broadcasted_iota(jnp.int32, (IMAGE, 1), 0) < size
    col = lax.broadcasted_iota(jnp.int32, (1, IMAGE), 1) < size
    row = jnp.where(row, 1, 0)
    col = jnp.where(col, 1, 0)
    return (row == col) | (block < TILES - 1)


def standard(value):
    centred = value - jnp.mean(value, axis=-1, keepdims=True)
    inverse = lax.rsqrt(jnp.mean(centred * centred, axis=-1, keepdims=True) + EPSILON)
    return centred * inverse, inverse


def norm_back(upper, xhat, inverse, gain):
    scaled = upper * gain
    return inverse * (
        scaled
        - jnp.mean(scaled, axis=-1, keepdims=True)
        - xhat * jnp.mean(scaled * xhat, axis=-1, keepdims=True)
    )


def add_up(ref, value):
    @pl.when(pl.program_id(0) == 0)
    def _():
        ref[...] = jnp.zeros_like(ref)

    ref[...] += value


def col_sum(value):
    return jnp.sum(value, axis=0, keepdims=True)


def params(limit=56):
    return pltpu.CompilerParams(
        dimension_semantics=("arbitrary",), vmem_limit_bytes=limit * 1024 * 1024
    )


def aligned(shift):
    return pl.multiple_of(lax.shift_left(lax.shift_right_logical(shift, 3), 3), 8)


def taken(scratch, shift):
    near = scratch[pl.ds(aligned(shift), IMAGE + 8), :]
    back_by = (IMAGE + 8) - (shift - aligned(shift))
    return pltpu.roll(near, back_by, 0)[:IMAGE]


def attend_kernel(shift_ref, xa, xb, ca, cb, w, vecs,
                  x_out, c_out, n_out, qkv_out, att_out, lse_out, scratch):
    block = pl.program_id(0)
    shift = shift_ref[0]
    scratch[0:IMAGE] = ca[...].astype(f32)
    scratch[IMAGE:2 * IMAGE] = cb[...].astype(f32)
    c_out[...] = taken(scratch, shift).astype(bf16)
    scratch[0:IMAGE] = xa[...].astype(f32)
    scratch[IMAGE:2 * IMAGE] = xb[...].astype(f32)
    x = taken(scratch, shift)
    x_out[...] = x.astype(bf16)
    xhat, _ = standard(x)
    normed = (xhat * vec(vecs, "g1") + vec(vecs, "b1")).astype(bf16)
    n_out[...] = normed
    qkv_out[...] = (dot(normed, w[...], NN) + vec(vecs, "bq")).astype(bf16)
    same = same_image(block, shift)
    sums = [jnp.zeros((IMAGE, 128), f32) for _ in range(D // 128)]
    marks = jnp.zeros((IMAGE, 128), f32)
    lane = lax.broadcasted_iota(jnp.int32, (1, 128), 1)
    for head in range(HEADS):
        first, start, width = window(head)
        mask = lane_mask(first, start, width)
        q = qkv_out[:, start:start + width]
        k = qkv_out[:, D + start:D + start + width]
        v = qkv_out[:, 2 * D + start:2 * D + start + width]
        q = jnp.where(mask, q, jnp.zeros_like(q))
        v = jnp.where(mask, v, jnp.zeros_like(v))
        scores = jnp.where(same, dot(q, k, NT), -1e30)
        highest = jnp.max(scores, axis=-1, keepdims=True)
        expo = jnp.exp2((scores - highest) * SCALE2)
        total = jnp.sum(expo, axis=-1, keepdims=True)
        probs = (expo * (1.0 / total)).astype(bf16)
        part = dot(probs, v, NN)
        for t in range(width // 128):
            at = start // 128 + t
            sums[at] = sums[at] + part[:, 128 * t:128 * t + 128]
        marks = jnp.where(lane == head, highest * SCALE2 + jnp.log2(total), marks)
    for t in range(D // 128):
        att_out[:, 128 * t:128 * t + 128] = sums[t].astype(bf16)
    lse_out[...] = marks


def attend(shift, tokens, cot, w, vecs):
    nxt = pl.BlockSpec((IMAGE, D), lambda b, *_: (lax.rem(b + 1, TILES), 0))
    return pl.pallas_call(
        attend_kernel,
        grid_spec=pltpu.PrefetchScalarGridSpec(
            num_scalar_prefetch=1, grid=(TILES,),
            in_specs=[rows(D), nxt, rows(D), nxt, whole((D, 3 * D)), whole((1, TOTAL))],
            out_specs=[rows(D), rows(D), rows(D), rows(3 * D), rows(D), rows(128)],
            scratch_shapes=[pltpu.VMEM((2 * IMAGE + 8, D), f32)]),
        out_shape=[jax.ShapeDtypeStruct((LENGTH, D), bf16)] * 3
        + [jax.ShapeDtypeStruct((LENGTH, 3 * D), bf16), jax.ShapeDtypeStruct((LENGTH, D), bf16),
           jax.ShapeDtypeStruct((LENGTH, 128), f32)],
        compiler_params=params(), name="attend",
    )(shift, tokens, tokens, cot, cot, w, vecs)


def gelu_pair(v):
    half = 0.5 * (1.0 + lax.erf(v * 0.7071067811865476))
    slope = jnp.exp2(v * v * (-0.5 * LOG2E)) * 0.3989422804014327
    return v * half, half + v * slope


def widen_kernel(x, att, wo, wu, vecs, after_out, n_out, hid_out, gp_out):
    after = x[...].astype(f32) + dot(att[...], wo[...], NN) + vec(vecs, "bo")
    after_out[...] = after
    xhat, _ = standard(after)
    normed = (xhat * vec(vecs, "g2") + vec(vecs, "b2")).astype(bf16)
    n_out[...] = normed
    for c in range(0, 4 * D, D):
        pre = dot(normed, wu[:, c:c + D], NN) + vec(vecs, "bu", c, D)
        value, slope = gelu_pair(pre)
        hid_out[:, c:c + D] = value.astype(bf16)
        gp_out[:, c:c + D] = slope.astype(bf16)


def widen(x, att, wo, wu, vecs):
    ff = wu.shape[1]
    return pl.pallas_call(
        widen_kernel, grid=(TILES,),
        in_specs=[rows(D), rows(D), whole((D, D)), whole((D, ff)), whole((1, TOTAL))],
        out_specs=[rows(D), rows(D), rows(ff), rows(ff)],
        out_shape=[jax.ShapeDtypeStruct((LENGTH, D), f32), jax.ShapeDtypeStruct((LENGTH, D), bf16),
                   jax.ShapeDtypeStruct((LENGTH, ff), bf16), jax.ShapeDtypeStruct((LENGTH, ff), bf16)],
        compiler_params=params(), name="widen",
    )(x, att, wo, wu, vecs)


def place(scratch, value, shift):
    near = aligned(shift)
    first = shift - near
    at = pl.multiple_of(pl.program_id(0) * IMAGE + near, 8)
    moved = pltpu.roll(jnp.concatenate([value, jnp.zeros((8, D), f32)]), first, 0)
    row = lax.broadcasted_iota(jnp.int32, (8, 1), 0)
    scratch[pl.ds(at, 8), :] = jnp.where(row < first, scratch[pl.ds(at, 8), :], moved[:8])
    scratch[pl.ds(pl.multiple_of(at + 8, 8), IMAGE), :] = moved[8:]


def wrapped(scratch, shift):
    row = lax.broadcasted_iota(jnp.int32, (IMAGE, 1), 0)
    return jnp.where(row < shift, scratch[LENGTH:LENGTH + IMAGE], scratch[:IMAGE])


def narrow_kernel(shift_ref, hid, gp, after, cot, wd, vecs, out, pre_out, bu_out, bd_out, scratch):
    shift = shift_ref[0]
    value = after[...] + dot(hid[...], wd[...], NN) + vec(vecs, "bd")
    place(scratch, value, shift)
    upper = cot[...]
    add_up(bd_out, col_sum(upper.astype(f32)))
    ff = hid.shape[1]

    @pl.when(pl.program_id(0) == 0)
    def _():
        bu_out[...] = jnp.zeros_like(bu_out)

    for c in range(0, ff, D):
        grad = dot(upper, wd[c:c + D, :], NT) * gp[:, c:c + D].astype(f32)
        grad = grad.astype(bf16)
        pre_out[:, c:c + D] = grad
        bu_out[:, c:c + D] += col_sum(grad.astype(f32))

    @pl.when(pl.program_id(0) == TILES - 1)
    def _():
        out[IMAGE:] = scratch[IMAGE:LENGTH].astype(bf16)
        out[:IMAGE] = wrapped(scratch, shift).astype(bf16)


def narrow(shift, hid, gp, after, cot, wd, vecs):
    ff = wd.shape[0]
    return pl.pallas_call(
        narrow_kernel,
        grid_spec=pltpu.PrefetchScalarGridSpec(
            num_scalar_prefetch=1, grid=(TILES,),
            in_specs=[rows(ff), rows(ff), rows(D), rows(D), whole((ff, D)), whole((1, TOTAL))],
            out_specs=[kept((LENGTH, D)), rows(ff), kept((1, ff)), kept((1, D))],
            scratch_shapes=[pltpu.VMEM((LENGTH + IMAGE + 8, D), f32)]),
        out_shape=[jax.ShapeDtypeStruct((LENGTH, D), bf16), jax.ShapeDtypeStruct((LENGTH, ff), bf16),
                   jax.ShapeDtypeStruct((1, ff), f32), jax.ShapeDtypeStruct((1, D), f32)],
        compiler_params=params(), name="narrow",
    )(shift, hid, gp, after, cot, wd, vecs)


def back_kernel(shift_ref, pre, after, cot, qkv, lse, wu, wo, vecs,
                ag_out, pg_out, dqkv_out, g2_out, b2_out, bo_out, bqkv_out):
    block = pl.program_id(0)
    shift = shift_ref[0]
    dn = dot(pre[...], wu[...], NT)
    xhat, inverse = standard(after[...])
    add_up(g2_out, col_sum(dn * xhat))
    add_up(b2_out, col_sum(dn))
    after_grad = cot[...].astype(f32) + norm_back(dn, xhat, inverse, vec(vecs, "g2"))
    ag_out[...] = after_grad
    proj = after_grad.astype(bf16)
    pg_out[...] = proj
    add_up(bo_out, col_sum(proj.astype(f32)))
    upper_all = dot(proj, wo[...], NT).astype(bf16)
    same = same_image(block, shift)
    count = D // 128
    sums = [[None] * count for _ in range(3)]
    for head in range(HEADS):
        first, start, width = window(head)
        mask = lane_mask(first, start, width)
        q = qkv[:, start:start + width]
        k = qkv[:, D + start:D + start + width]
        v = qkv[:, 2 * D + start:2 * D + start + width]
        u = upper_all[:, start:start + width]
        q = jnp.where(mask, q, jnp.zeros_like(q))
        k = jnp.where(mask, k, jnp.zeros_like(k))
        u = jnp.where(mask, u, jnp.zeros_like(u))
        scores = dot(q, k, NT)
        probs = jnp.exp2(scores * SCALE2 - lse[:, head:head + 1])
        probs = jnp.where(same, probs, 0.0)
        pgrad = dot(u, v, NT)
        centre = jnp.sum(probs * pgrad, axis=-1, keepdims=True)
        sg = (probs * (pgrad - centre)).astype(bf16)
        parts = (dot(sg, k, NN), dot(sg, q, TN), dot(probs.astype(bf16), u, TN))
        for which in range(3):
            for t in range(width // 128):
                at = start // 128 + t
                piece = parts[which][:, 128 * t:128 * t + 128]
                old = sums[which][at]
                sums[which][at] = piece if old is None else old + piece
    for which in range(3):
        for t in range(count):
            value = sums[which][t]
            if which < 2:
                value = value * HEAD_DIM ** (-0.5)
            dqkv_out[:, which * D + 128 * t:which * D + 128 * t + 128] = value.astype(bf16)
    add_up(bqkv_out, col_sum(dqkv_out[...].astype(f32)))


def back(shift, pre, after, cot, qkv, lse, wu, wo, vecs):
    ff = wu.shape[1]
    row = jax.ShapeDtypeStruct((1, D), f32)
    return pl.pallas_call(
        back_kernel,
        grid_spec=pltpu.PrefetchScalarGridSpec(
            num_scalar_prefetch=1, grid=(TILES,),
            in_specs=[rows(ff), rows(D), rows(D), rows(3 * D), rows(128), whole((D, ff)),
                      whole((D, D)), whole((1, TOTAL))],
            out_specs=[rows(D), rows(D), rows(3 * D), kept((1, D)), kept((1, D)), kept((1, D)),
                       kept((1, 3 * D))]),
        out_shape=[jax.ShapeDtypeStruct((LENGTH, D), f32), jax.ShapeDtypeStruct((LENGTH, D), bf16),
                   jax.ShapeDtypeStruct((LENGTH, 3 * D), bf16), row, row, row,
                   jax.ShapeDtypeStruct((1, 3 * D), f32)],
        compiler_params=params(), name="back",
    )(shift, pre, after, cot, qkv, lse, wu, wo, vecs)


def entry_kernel(shift_ref, dqkv, x, ag, w, vecs, tg_out, g1_out, b1_out, scratch):
    shift = shift_ref[0]
    dn = dot(dqkv[...], w[...], NT)
    xhat, inverse = standard(x[...].astype(f32))
    add_up(g1_out, col_sum(dn * xhat))
    add_up(b1_out, col_sum(dn))
    place(scratch, ag[...] + norm_back(dn, xhat, inverse, vec(vecs, "g1")), shift)

    @pl.when(pl.program_id(0) == TILES - 1)
    def _():
        tg_out[IMAGE:] = scratch[IMAGE:LENGTH]
        tg_out[:IMAGE] = wrapped(scratch, shift)


def entry(shift, dqkv, x, ag, w, vecs):
    row = jax.ShapeDtypeStruct((1, D), f32)
    return pl.pallas_call(
        entry_kernel,
        grid_spec=pltpu.PrefetchScalarGridSpec(
            num_scalar_prefetch=1, grid=(TILES,),
            in_specs=[rows(3 * D), rows(D), rows(D), whole((D, 3 * D)), whole((1, TOTAL))],
            out_specs=[kept((LENGTH, D)), kept((1, D)), kept((1, D))],
            scratch_shapes=[pltpu.VMEM((LENGTH + IMAGE + 8, D), f32)]),
        out_shape=[jax.ShapeDtypeStruct((LENGTH, D), f32), row, row],
        compiler_params=params(), name="entry",
    )(shift, dqkv, x, ag, w, vecs)


def product(left, right):
    return lax.dot_general(left, right, (TN, ((), ())), preferred_element_type=f32).astype(bf16)


def swap(value, flip, size):
    return lax.ppermute(value, "narrow", [(a, a ^ flip) for a in range(size)])


def both(first, second):
    return (first.astype(f32) + second.astype(f32)).astype(bf16)


def pick(value, index, axis):
    return lax.dynamic_index_in_dim(value, index, axis, keepdims=False)


def half(value, index):
    size = value.shape[1] // 2
    return lax.dynamic_slice_in_dim(value, index * size, size, 1)


def reduced(left, right, wide):
    place_n = lax.axis_index("narrow")
    core, side = place_n % 2, place_n // 2
    sent = product(left, half(right, 1 - core))
    arrived = swap(sent, 1, 4)
    own = product(left, half(right, core))
    cut = (wide, 2, own.shape[0] // (2 * wide), own.shape[1])
    own, arrived = own.reshape(cut), arrived.reshape(cut)
    moving = both(pick(own, 1 - side, 1), pick(arrived, 1 - side, 1))
    met = swap(moving, 2, 4)
    total = pick(own, side, 1).astype(f32) + pick(arrived, side, 1).astype(f32) + met.astype(f32)
    parts = lax.all_to_all(total.astype(bf16), "wide", split_axis=0, concat_axis=0, tiled=True)
    mine = jnp.sum(parts.astype(f32), axis=0).astype(bf16)
    every = lax.all_gather(mine, "narrow", axis=0, tiled=False)
    every = every.reshape(2, 2, cut[2], cut[3]).transpose(0, 2, 1, 3)
    return every.reshape(2 * cut[2], 2 * cut[3]).astype(f32)


def shards(wide, tokens, segment_ids, cotangent, ln1_gain, ln1_bias, qkv_weight, qv_bias,
           out_weight, out_bias, ln2_gain, ln2_bias, up_weight, up_bias, down_weight, down_bias):
    def gathered(value):
        return lax.all_gather(value, "wide", axis=0, tiled=True)

    small = jnp.concatenate([ln1_gain, ln1_bias, qv_bias, out_bias, ln2_gain, ln2_bias, up_bias, down_bias])
    small = lax.all_gather(small, "wide", axis=0, tiled=False).astype(f32)
    flat = []
    at = 0
    for value in (ln1_gain, ln1_bias, qv_bias, out_bias, ln2_gain, ln2_bias, up_bias, down_bias):
        flat.append(small[:, at:at + value.shape[0]].reshape(-1))
        at += value.shape[0]
    flat[2:3] = [flat[2][:D], jnp.zeros((D,), f32), flat[2][D:]]
    vecs = jnp.concatenate(flat).reshape(1, TOTAL)
    shift = jnp.sum((segment_ids == 0).astype(jnp.int32)).reshape(1)
    wq = gathered(qkv_weight)
    wo = gathered(out_weight)
    wu = gathered(up_weight)
    wd = gathered(down_weight)
    x, cot, first, qkv, att, lse = attend(shift, tokens, cotangent, wq, vecs)
    after, second, hid, gp = widen(x, att, wo, wu, vecs)
    down_grad = reduced(hid, cot, wide)
    out, pre, gbu, gbd = narrow(shift, hid, gp, after, cot, wd, vecs)
    up_grad = reduced(second, pre, wide)
    ag, proj, dqkv, gg2, gb2, gbo, gbq = back(shift, pre, after, cot, qkv, lse, wu, wo, vecs)
    out_grad = reduced(att, proj, wide)
    qkv_grad = reduced(first, dqkv, wide)
    tokens_grad, gg1, gb1 = entry(shift, dqkv, x, ag, wq, vecs)
    sums = jnp.concatenate([gg1, gb1, gbq[:, :D], gbq[:, 2 * D:], gbo, gg2, gb2, gbu, gbd], axis=1)[0]
    sums = lax.psum(sums, ("wide", "narrow"))
    index = lax.axis_index("wide")
    grads = []
    at = 0
    for value in (ln1_gain, ln1_bias, qv_bias, out_bias, ln2_gain, ln2_bias, up_bias, down_bias):
        size = value.shape[0]
        grads.append(lax.dynamic_slice_in_dim(sums, at + index * size, size))
        at += size * wide
    g1, b1, bq, bo, g2, b2, bu, bd = grads
    return (out, tokens_grad, g1, b1, qkv_grad, bq, out_grad, bo, g2, b2, up_grad, bu, down_grad, bd)


def solution(mesh):
    wide = mesh.shape["wide"]
    token = P(("wide", "narrow"), None)
    row, flat = P("wide", None), P("wide")
    ins = (token, P(("wide", "narrow")), token, flat, flat, row, flat, row, flat, flat, flat, row, flat, row, flat)
    outs = (token, token, flat, flat, row, flat, row, flat, flat, flat, row, flat, row, flat)
    return jax.shard_map(functools.partial(shards, wide), mesh=mesh, in_specs=ins, out_specs=outs, check_vma=False)
```
